32 devices in a mesh: groups: 2 (over y), dom: 4 (over x, core), shard: 4 (over z).
Axes of the slice: x: 2, y: 2, z: 4, core: 2. Of those that a mesh axis runs over, the one named last changes fastest.
Arguments:
- rows: float32 [8, 8, 1152], P(('groups', 'dom'), 'shard'), parts along dimension 0, may hold values from -6 to 6
- targets: float32 [8, 8, 1152], P(('groups', 'dom'), 'shard'), parts along dimension 0, may hold values from -6 to 6
- w_gate: bfloat16 [4, 4608, 1152], P('dom', 'shard'), may hold values from -6 to 6
- w_up: bfloat16 [4, 4608, 1152], P('dom', 'shard'), may hold values from -6 to 6
- w_down: bfloat16 [4, 4608, 1152], P('dom', 'shard'), may hold values from -6 to 6
- member_at: int32 [2, 4], replicated, may hold values from 0 to 3, as said below
- lr_index: int32 [4], replicated, may hold values from 0 to 3
- rates: float32 [4], replicated, may hold values from 0.25 to 2
Outputs:
- pred: float32 [8, 8, 1152], P(('groups', 'dom'), 'shard'), parts along dimension 0
- grad_in: float32 [8, 8, 1152], P(('groups', 'dom'), 'shard'), parts along dimension 0
- new_gate: bfloat16 [8, 4608, 1152], P(('groups', 'dom'), 'shard'), parts along dimension 0
- new_up: bfloat16 [8, 4608, 1152], P(('groups', 'dom'), 'shard'), parts along dimension 0
- new_down: bfloat16 [8, 4608, 1152], P(('groups', 'dom'), 'shard'), parts along dimension 0
The draws below stay inside these ranges and needn't reach their ends.
There are 2 independent parts, one for each index of `groups`. The reference program is written for one: setup_inputs(seed, part) draws one part's arguments, and reference() takes and returns one part's arrays. A program takes and returns all parts, laid end to end along the dimension named above; an argument that names none is the same for every part. Nothing has to cross between parts.
Inputs may be any that keep to these rules, and one draw needn't show every extreme that they name: Row 0 is a permutation of the members, and member_at[h, p] = member_at[0, (p - h) mod 4]: each member moves to the next partition at every step.
All inputs are finite; a program needn't handle non-finite values.
Results may differ from the reference program's by a relative error of at most 0.011.
Values may be sent and summed in bfloat16 or wider, within the bound.
No kernel may reach another device: no remote copies, remote signals or barrier semaphores. Data moves between devices by JAX's collectives and lax.ppermute only.
A program may use at most 64 MiB of HBM per device.

```python
import math
import jax
import jax.numpy as jnp

D = 1152
FF = 4608
HOPS = 2
RATES = 4
MEMBERS = 4
ROWS = 8


def draw_member_at(key, part):
    order = jax.random.permutation(key, MEMBERS)
    where_from = (jnp.arange(MEMBERS)[None, :] - jnp.arange(HOPS)[:, None]) % MEMBERS
    return order[where_from].astype(jnp.int32)


def place_ends(drawn, rng, smallest, high):
    spot = [jax.random.randint(jax.random.fold_in(rng, axis), (), 0, length) for axis, length in enumerate(drawn.shape)]
    widest = drawn.shape.index(max(drawn.shape))
    neighbour = spot[:widest] + [(spot[widest] + 1) % drawn.shape[widest]] + spot[widest + 1:]
    return drawn.at[tuple(spot)].set(smallest).at[tuple(neighbour)].set(high)


def block_scale(own_key, shape, pieces, smallest, largest):
    loudness = 1.0
    for axis_at, parts in pieces:
        heights = jax.random.uniform(jax.random.fold_in(jax.random.fold_in(own_key, 6), axis_at), (parts,), jnp.float32, smallest / len(pieces), largest / len(pieces))
        loudness = loudness * jnp.repeat(jnp.exp(heights), shape[axis_at] // parts).reshape((-1,) + (1,) * (len(shape) - 1 - axis_at))
    return loudness


def centred(stream_key, extent, spread, most, shards=(), kind=jnp.bfloat16):
    loudness = block_scale(stream_key, extent, shards, -0.22, 0.18) if shards else 1.0
    drawn = jax.random.normal(stream_key, extent, jnp.float32) * spread * loudness
    return jnp.minimum(jnp.maximum(drawn, -most), most).astype(kind)


def setup_inputs(seed: int = 0, part: int = 0) -> dict:
    key_of = jax.random.split(jax.random.key(seed), 9)
    part_keys = jax.random.split(jax.random.fold_in(key_of[8], part), 9)
    return {
        "rows": centred(part_keys[0], (MEMBERS, ROWS, D), 1.0, 6.0, ((0, 4), (1, 4)), jnp.float32),
        "targets": centred(part_keys[1], (MEMBERS, ROWS, D), 1.0, 6.0, ((0, 4), (1, 4)), jnp.float32),
        "w_gate": centred(key_of[2], (MEMBERS, FF, D), 1.0, 6.0, ((0, 4), (1, 4))),
        "w_up": centred(key_of[3], (MEMBERS, FF, D), 1.0, 6.0, ((0, 4), (1, 4))),
        "w_down": centred(key_of[4], (MEMBERS, FF, D), 1.0, 6.0, ((0, 4), (1, 4))),
        "member_at": draw_member_at(jax.random.fold_in(key_of[8], 71), part),
        "lr_index": place_ends(jax.random.randint(key_of[6], (MEMBERS,), 0, RATES), jax.random.fold_in(key_of[6], 1), 0, RATES - 1).astype(jnp.int32),
        "rates": jnp.clip(jnp.exp(jax.random.uniform(key_of[7], (RATES,), jnp.float32, math.log(0.25), math.log(2.0))), 0.25, 2.0),
    }


def train_member(inputs, target, gate_w, up_w, down_w, step_rate):
    scale_in = D ** -0.5
    scale_hidden = FF ** -0.5
    gate = jnp.dot(inputs, gate_w.T, preferred_element_type=jnp.float32) * scale_in
    upward = jnp.dot(inputs, up_w.T, preferred_element_type=jnp.float32) * scale_in
    sigma = jax.nn.sigmoid(gate)
    hidden = (gate * sigma * upward).astype(jnp.bfloat16)
    output = jnp.dot(hidden, down_w, preferred_element_type=jnp.float32) * scale_hidden
    resid_b = (output - target).astype(jnp.bfloat16)
    d_hidden = jnp.dot(resid_b, down_w.T, preferred_element_type=jnp.float32) * scale_hidden
    d_gate = (d_hidden * upward * sigma * (1.0 + gate * (1.0 - sigma))).astype(jnp.bfloat16)
    d_upward = (d_hidden * gate * sigma).astype(jnp.bfloat16)
    grad_down = jnp.dot(hidden.T, resid_b, preferred_element_type=jnp.float32) * scale_hidden
    grad_gate = jnp.dot(d_gate.T, inputs, preferred_element_type=jnp.float32) * scale_in
    grad_up = jnp.dot(d_upward.T, inputs, preferred_element_type=jnp.float32) * scale_in
    d_inputs = (jnp.dot(d_gate, gate_w, preferred_element_type=jnp.float32)
                + jnp.dot(d_upward, up_w, preferred_element_type=jnp.float32)) * scale_in
    new_gate = (gate_w.astype(jnp.float32) - step_rate * grad_gate).astype(jnp.bfloat16)
    new_up = (up_w.astype(jnp.float32) - step_rate * grad_up).astype(jnp.bfloat16)
    new_down = (down_w.astype(jnp.float32) - step_rate * grad_down).astype(jnp.bfloat16)
    return output, d_inputs, new_gate, new_up, new_down


def reference(rows, targets, w_gate, w_up, w_down, member_at, lr_index, rates):
    inputs = rows.astype(jnp.bfloat16)
    gates, ups, downs = w_gate, w_up, w_down
    preds = []
    grads = []
    for hop_index in range(HOPS):
        outs_gate = []
        outs_up = []
        outs_down = []
        preds = []
        grads = []
        for part_index in range(MEMBERS):
            step_rate = rates[lr_index[member_at[hop_index, part_index]]]
            output, d_inputs, new_gate, new_up, new_down = train_member(
                inputs[part_index], targets[part_index], gates[part_index], ups[part_index],
                downs[part_index], step_rate)
            preds.append(output)
            grads.append(d_inputs)
            outs_gate.append(new_gate)
            outs_up.append(new_up)
            outs_down.append(new_down)
        gates = jnp.roll(jnp.stack(outs_gate), 1, axis=0)
        ups = jnp.roll(jnp.stack(outs_up), 1, axis=0)
        downs = jnp.roll(jnp.stack(outs_down), 1, axis=0)
    return jnp.stack(preds), jnp.stack(grads), gates, ups, downs
```

```python
import functools

import jax
import jax.numpy as jnp
from jax import lax
from jax.experimental import pallas as pl
from jax.experimental.pallas import tpu as pltpu
from jax.sharding import PartitionSpec as P


BLOCK = 128
SMALL_RING = 8


def shifted(value, axis, steps):
    count = lax.axis_size(axis)
    pairs = [(source, (source + steps) % count) for source in range(count)]
    return lax.ppermute(value, axis, pairs)


def gathered_rows(value):
    count = lax.axis_size("shard")
    if count > SMALL_RING:
        return lax.all_gather(value, "shard", axis=0, tiled=True)
    parts = [value]
    for step in range(1, count):
        parts.append(shifted(value, "shard", step))
    return jnp.concatenate(parts, axis=0)


def summed_rows(partial):
    count = lax.axis_size("shard")
    if count > SMALL_RING:
        return lax.psum(partial, "shard")
    own = partial.shape[0] // count
    total = partial
    for step in range(1, count):
        got = shifted(partial, "shard", step)
        total = total + jnp.roll(got, step * own, axis=0)
    return total


def own_rows(full):
    count = lax.axis_size("shard")
    own = full.shape[0] // count
    if count > SMALL_RING:
        return lax.dynamic_slice_in_dim(full, lax.axis_index("shard") * own, own, 0)
    return full[:own]


def summed_own_rows(partial):
    count = lax.axis_size("shard")
    if count > SMALL_RING:
        return lax.psum_scatter(partial, "shard", scatter_dimension=0, tiled=True)
    own = partial.shape[0] // count
    total = partial[:own]
    for step in range(1, count):
        at = (count - step) * own
        total = total + shifted(partial[at : at + own], "shard", step)
    return total


def lookup(table, wanted):
    positions = jnp.arange(table.shape[0], dtype=jnp.int32)
    return jnp.sum(jnp.where(positions == wanted, table, jnp.zeros_like(table)))


def rate_of(member_at, lr_index, rates, step, partition):
    member = lookup(member_at[step], partition)
    return lookup(rates, lookup(lr_index, member))


def dot(a, b, dims):
    return lax.dot_general(a, b, (dims, ((), ())), preferred_element_type=jnp.float32)


def stepped(weight, left, right, rate):
    grad = dot(left, right, ((0,), (0,)))
    return (weight.astype(jnp.float32) - rate * grad).astype(jnp.bfloat16)


def block_kernel(entries, hops, left_at, right_at, at_ref, rate_ref, *refs):
    count = len(entries)
    packs, blocks = refs[:hops], refs[hops : hops + count]
    wide = blocks[0].shape[1]
    out_ref, done, sems = refs[-3:]
    copies = []
    for index, (first, second) in enumerate(entries):
        at = jnp.where(at_ref[0] == 0, first, second)
        start = pl.multiple_of(at * BLOCK, BLOCK)
        value = blocks[index][...]
        for hop in range(hops):
            left = packs[hop][:, pl.ds(pl.multiple_of(left_at + start, BLOCK), BLOCK)]
            right = packs[hop][:, right_at : right_at + wide]
            value = stepped(value, left, right, rate_ref[hop])
        done[index] = value
        copy = pltpu.make_async_copy(
            done.at[index], out_ref.at[pl.ds(start, BLOCK), :], sems.at[index]
        )
        copy.start()
        copies.append(copy)
    for copy in copies:
        copy.wait()


def updated_blocks(at, rate, packs, sides, blocks, entries, shape, before=None):
    hops = len(packs)
    vmem = pl.BlockSpec(memory_space=pltpu.VMEM)
    smem = pl.BlockSpec(memory_space=pltpu.SMEM)
    anywhere = pl.BlockSpec(memory_space=pl.ANY)
    count = len(blocks)
    carried = [] if before is None else [before]
    return pl.pallas_call(
        functools.partial(block_kernel, entries, hops, *sides),
        out_shape=jax.ShapeDtypeStruct(shape, jnp.bfloat16),
        in_specs=[smem, smem] + [vmem] * (hops + count) + [anywhere] * len(carried),
        out_specs=anywhere,
        scratch_shapes=[
            pltpu.VMEM((count, BLOCK, shape[1]), jnp.bfloat16),
            pltpu.SemaphoreType.DMA((count,)),
        ],
        input_output_aliases={} if before is None else {2 + hops + count: 0},
        cost_estimate=pl.CostEstimate(
            flops=4 * hops * count * BLOCK * shape[1] * packs[0].shape[0],
            bytes_accessed=4 * count * BLOCK * shape[1],
            transcendentals=0,
        ),
        compiler_params=pltpu.CompilerParams(vmem_limit_bytes=24 * 2**20),
        name="apply_steps",
    )(at, rate, *packs, *blocks, *carried)


def forward(inputs, weights):
    gate_w, up_w, down_w = weights
    scale_in = gate_w.shape[1] ** (-0.5)
    gate = dot(inputs, gate_w, ((1,), (1,))) * scale_in
    upward = dot(inputs, up_w, ((1,), (1,))) * scale_in
    sigma = jax.nn.sigmoid(gate)
    hidden = (gate * sigma * upward).astype(jnp.bfloat16)
    partial_out = dot(hidden, down_w, ((1,), (0,)))
    return gate, upward, sigma, hidden, partial_out


def backward(resid, down_w, gate, upward, sigma, scale_hidden):
    d_hidden = dot(resid, down_w, ((1,), (1,))) * scale_hidden
    d_gate = (d_hidden * upward * sigma * (1.0 + gate * (1.0 - sigma))).astype(jnp.bfloat16)
    d_upward = (d_hidden * gate * sigma).astype(jnp.bfloat16)
    return d_gate, d_upward


def local(rows, targets, w_gate, w_up, w_down, member_at, lr_index, rates):
    return local_body(
        rows[0], targets[0], (w_gate[0], w_up[0], w_down[0]), member_at, lr_index, rates
    )


def local_body(rows, targets, weights, member_at, lr_index, rates):
    hops = member_at.shape[0]
    parts = lax.axis_size("dom")
    position = lax.axis_index("dom")
    group = lax.axis_index("groups")
    tall, wide = weights[0].shape
    hidden_units = tall * lax.axis_size("shard")
    scale_in = wide ** (-0.5)
    scale_hidden = hidden_units ** (-0.5)
    start = weights
    relayed = lax.axis_size("groups") == 2 and tall % BLOCK == 0 and tall >= BLOCK

    local_data = jnp.concatenate([rows, targets], axis=0)
    own = rows.shape[0]
    visits = [local_data]
    for hop in range(1, hops):
        visits.append(shifted(local_data, "dom", -hop))

    nblocks = tall // BLOCK if relayed else 0
    pairs, arrived = [], []
    if relayed:
        leftovers = [(m, nblocks - 1) for m in range(3)] if nblocks % 2 else []
        pairs = [((m, 2 * j), (m, 2 * j + 1)) for m in range(3) for j in range(nblocks // 2)]
        if leftovers:
            pairs.insert(2 * (nblocks // 2), (leftovers[0], leftovers[1]))
        direct = leftovers[2:]

        def block(which):
            m, b = which
            return lax.slice_in_dim(start[m], b * BLOCK, (b + 1) * BLOCK, axis=0)

        for first, second in pairs:
            if first[0] == second[0]:
                mine = lax.dynamic_slice_in_dim(
                    start[first[0]], (first[1] + group) * BLOCK, BLOCK, 0
                )
            else:
                mine = jnp.where(group == 0, block(first), block(second))
            got = shifted(mine, "dom", hops)
            other = shifted(got, "groups", 1)
            arrived.append((got, other))
        directly = []
        for which in direct:
            directly.append(shifted(block(which), "dom", hops))

    packs = []
    for hop in range(hops):
        last = hop == hops - 1
        data = gathered_rows(visits[hop])
        count = data.shape[0] // (2 * own)
        data = data.reshape(count, 2, own, wide)
        inputs = data[:, 0].reshape(count * own, wide).astype(jnp.bfloat16)
        wanted = data[:, 1].reshape(count * own, wide)
        gate, upward, sigma, hidden, partial_out = forward(inputs, weights)
        output = summed_rows(partial_out * scale_hidden)
        resid = (output - wanted).astype(jnp.bfloat16)
        d_gate, d_upward = backward(resid, weights[2], gate, upward, sigma, scale_hidden)
        packs.append(jnp.concatenate([d_gate, d_upward, hidden, inputs, resid], axis=1))
        if not last:
            rate = rate_of(member_at, lr_index, rates, hop, (position + hop) % parts)
            weights = (
                stepped(weights[0], d_gate, inputs, rate * scale_in),
                stepped(weights[1], d_upward, inputs, rate * scale_in),
                stepped(weights[2], hidden, resid, rate * scale_hidden),
            )
        else:
            d_partial = (
                dot(d_gate, weights[0], ((1,), (0,))) + dot(d_upward, weights[1], ((1,), (0,)))
            ) * scale_in
            grad_own = summed_own_rows(d_partial)
            results = jnp.concatenate([own_rows(output), grad_own], axis=0)
            results = shifted(results, "dom", hops - 1)
    came = []
    for hop in range(hops):
        came.append(shifted(packs[hop], "dom", hops))

    home = (position - hops) % parts
    rate = jnp.stack(
        [rate_of(member_at, lr_index, rates, hop, (home + hop) % parts) for hop in range(hops)]
    )
    scales = (scale_in, scale_in, scale_hidden)
    sides = tuple((m * tall, 3 * tall + (m // 2) * wide) for m in range(3))
    news = []
    if relayed:
        at = group.reshape(1).astype(jnp.int32)
        for m in range(3):
            blocks, entries = [], []
            for (first, second), (got, other) in zip(pairs, arrived):
                if first[0] == second[0] == m:
                    blocks += [got, other]
                    entries += [(first[1], second[1]), (second[1], first[1])]
                elif first[0] == m:
                    blocks.append(jnp.where(group == 0, got, other))
                    entries.append((first[1], first[1]))
                elif second[0] == m:
                    blocks.append(jnp.where(group == 0, other, got))
                    entries.append((second[1], second[1]))
            for which, got in zip(direct, directly):
                if which[0] == m:
                    blocks.append(got)
                    entries.append((which[1], which[1]))
            cut = len(blocks) - 3 if m == 2 and len(blocks) > 3 else len(blocks)
            new = updated_blocks(
                at, rate * scales[m], came, sides[m], blocks[:cut], entries[:cut], (tall, wide)
            )
            if cut < len(blocks):
                new = updated_blocks(
                    at, rate * scales[m], came, sides[m], blocks[cut:], entries[cut:], (tall, wide), new
                )
            news.append(new)
    else:
        for m in range(3):
            new = shifted(start[m], "dom", hops)
            for hop in range(hops):
                left_at, right_at = sides[m]
                left = came[hop][:, left_at : left_at + tall]
                right = came[hop][:, right_at : right_at + wide]
                new = stepped(new, left, right, rate[hop] * scales[m])
            news.append(new)
    return (results[None, :own], results[None, own:], news[0][None], news[1][None], news[2][None])


def solution(mesh):
    return jax.shard_map(
        local,
        mesh=mesh,
        in_specs=(
            P(("groups", "dom"), "shard", None),
            P(("groups", "dom"), "shard", None),
            P("dom", "shard", None),
            P("dom", "shard", None),
            P("dom", "shard", None),
            P(),
            P(),
            P(),
        ),
        out_specs=(P(("groups", "dom"), "shard", None),) * 5,
        check_vma=False,
    )
```
